32 devices in a mesh: rep: 2 (over x), walk: 16 (over z, y, core).
Axes of the slice: x: 2, y: 2, z: 4, core: 2. Of those that a mesh axis runs over, the one named last changes fastest.
Arguments:
- greens: bfloat16 [32, 64, 384], P(('rep', 'walk')), parts along dimension 0, may hold values from -6 to 6
- source: int32 [64], P(('rep', 'walk')), parts along dimension 0, may hold values from 0 to 15, as said below
- counts: int32 [32], P('rep'), parts along dimension 0, may hold values from 1 to 2, as said below
- cholesky: bfloat16 [512, 64, 384], P('walk'), may hold values from -0.0390625 to 0.0390625
Outputs:
- relocated: bfloat16 [64, 64, 384], P(('rep', 'walk')), parts along dimension 0
- exchange_energy: float32 [64], P(('rep', 'walk')), parts along dimension 0
- force_bias: float32 [64, 512], P(('rep', 'walk')), parts along dimension 0
The draws below stay inside these ranges and needn't reach their ends.
There are 2 independent parts, one for each index of `rep`. The reference program is written for one: setup_inputs(seed, part) draws one part's arguments, and reference() takes and returns one part's arrays. A program takes and returns all parts, laid end to end along the dimension named above; an argument that names none is the same for every part. Nothing has to cross between parts.
Inputs may be any that keep to these rules, and one draw needn't show every extreme that they name: `source`: slot s belongs to walk device s div 2. Its walker comes from that device or one of the two devices beside it along the closed loop of walk devices. Slots beyond a device's count also name some walker. Slots 0 to counts[d] - 1 of device d are live.
All inputs are finite; a program needn't handle non-finite values.
Results may differ from the reference program's by a relative error of at most 0.001.
Values may be sent and summed in bfloat16 or wider, within the bound.
A program may use at most 64 MiB of HBM per device.

```python
import jax
import jax.numpy as jnp
from jax import lax

NOCC = 64
NORB = 384
WSLOT = 1
CAP = 2
NW = 16
NW2 = 32
NCHOL = 512
N_WALK = 16


def population(key):
    base_key = jax.random.fold_in(key, 11)
    k_count, k_full, k_offset, k_local = jax.random.split(base_key, 4)
    counts = jax.random.randint(k_count, (N_WALK,), WSLOT, 2 * WSLOT + 1)
    fullest = jax.random.randint(k_full, (), 0, N_WALK)
    counts = counts.at[fullest].set(2 * WSLOT)
    counts = counts.at[(fullest + 1) % N_WALK].set(WSLOT)
    owner = jnp.arange(NW2) // CAP
    offset = jax.random.randint(k_offset, (NW2,), -1, 2)
    offset = offset.at[0].set(-1)
    offset = offset.at[CAP].set(-1)
    src_dev = (owner + offset) % N_WALK
    local_idx = jax.random.randint(k_local, (NW2,), 0, WSLOT)
    local_idx = local_idx.at[0].set(WSLOT - 1)
    local_idx = local_idx.at[CAP].set(0)
    source = (src_dev * WSLOT + local_idx).astype(jnp.int32)
    return (counts.astype(jnp.int32), source)


def draw_source(key, part):
    return population(key)[1]


def draw_counts(key, part):
    return population(key)[0]


def steps_of(own_key, shape, cuts, low, top_value):
    gain, own = 1.0, jax.random.fold_in(own_key, 6)
    for dim, blocks in cuts:
        draws = jnp.exp(jax.random.uniform(jax.random.fold_in(own, dim), (blocks,), jnp.float32, low / len(cuts), top_value / len(cuts)))
        gain = gain * jnp.repeat(draws, shape[dim] // blocks).reshape([-1 if axis == dim else 1 for axis in range(len(shape))])
    return gain


def normal_values(own_key, extent, scale, limit, pieces=(), held_as=jnp.bfloat16):
    gain = steps_of(own_key, extent, pieces, -0.22, 0.18) if pieces else 1.0
    values = jax.random.normal(own_key, extent, jnp.float32) * scale * gain
    return jnp.minimum(jnp.maximum(values, -limit), limit).astype(held_as)


def setup_inputs(seed: int = 0, part: int = 0) -> dict:
    keys = jax.random.split(jax.random.key(seed), 5)
    own_keys = jax.random.split(jax.random.fold_in(keys[4], part), 5)
    return {
        "greens": normal_values(own_keys[0], (NW, NOCC, NORB), 1.0, 6.0, ((0, 16),)),
        "source": draw_source(jax.random.fold_in(jax.random.fold_in(keys[4], part), 71), part),
        "counts": draw_counts(jax.random.fold_in(jax.random.fold_in(keys[4], part), 71), part),
        "cholesky": normal_values(keys[3], (NCHOL, NOCC, NORB), (NOCC * NORB) ** -0.5, 0.0390625, ((0, 16),)),
    }


def reference(greens, source, counts, cholesky):
    slot_pos = jnp.arange(NW2) % CAP
    owner = jnp.arange(NW2) // CAP
    is_live = slot_pos < counts[owner]
    relocated = jnp.where(is_live[:, None, None], greens[source], jnp.zeros((), jnp.bfloat16)).astype(jnp.bfloat16)
    chol_flat = cholesky.reshape(NCHOL * NOCC, NORB)

    def walker_energy(walker):
        rotated = jnp.dot(chol_flat, walker.T, preferred_element_type=jnp.float32).reshape(NCHOL, NOCC, NOCC)
        return -(0.5 / NCHOL) * jnp.sum(rotated * jnp.swapaxes(rotated, 1, 2))

    exchange_energy = lax.map(walker_energy, relocated)
    force_bias = jnp.dot(relocated.reshape(NW2, NOCC * NORB), cholesky.reshape(NCHOL, NOCC * NORB).T, preferred_element_type=jnp.float32)
    return relocated, exchange_energy, force_bias
```

```python
import functools

import jax
import jax.numpy as jnp
from jax import lax
from jax.experimental import pallas as pl
from jax.experimental.pallas import tpu as pltpu
from jax.sharding import PartitionSpec as P

MESH = pl.DeviceIdType.MESH
NEAR = 3
TILE = 4
STEP = 8


def flip(index, mask):
    bit = 1
    while bit <= mask:
        if mask & bit:
            index = index + bit - 2 * bit * ((index // bit) % 2)
        bit *= 2
    return index


def place(k, s):
    return 2 * k + s


def kernel(
    n, nocc, chol_dev, nchol,
    source_ref, counts_ref, greens_ref, chol_ref,
    reloc_ref, energy_ref, bias_ref,
    walkers, chol, near_by, diag, message, inbox,
    local_sem, line_send, pair_send, core_send, chol_recv, walker_recv, near_recv, mail_send, mail_recv,
):
    me = lax.axis_index("walk")
    depth = n // 4
    half = n // 2
    core = me % 2
    side = (me // 2) % 2
    z = me // 4
    chip = me // 2
    rows = chol_dev * nocc

    def device_of(zz, ss, cc):
        return (zz * 2 + ss) * 2 + cc

    sibling = device_of(z, side, 1 - core)
    partner = device_of(z, 1 - side, core)
    line = [device_of(flip(z, k), side, core) for k in range(depth)]

    load_own = pltpu.make_async_copy(greens_ref, walkers.at[0], local_sem.at[0])
    load_own.start()
    load_chol = pltpu.make_async_copy(chol_ref, chol.at[core], local_sem.at[1])
    load_chol.start()

    barrier = pltpu.get_barrier_semaphore()
    for other in [sibling, partner] + line[1:]:
        pl.semaphore_signal(barrier, inc=1, device_id={"walk": other}, device_id_type=MESH)
    diag[...] = jnp.zeros_like(diag)
    load_own.wait()
    pl.semaphore_wait(barrier, depth + 1)

    sent = []

    def send(src, dst, send_sem, recv_sem, target):
        copy = pltpu.make_async_remote_copy(
            src_ref=src,
            dst_ref=dst,
            send_sem=send_sem,
            recv_sem=recv_sem,
            device_id={"walk": target},
            device_id_type=MESH,
        )
        copy.start()
        sent.append(copy)

    def await_copy(ref, sem):
        pltpu.make_async_remote_copy(
            src_ref=ref,
            dst_ref=ref,
            send_sem=local_sem.at[0],
            recv_sem=sem,
            device_id={"walk": me},
            device_id_type=MESH,
        ).wait_recv()

    def to_slot(src, dst, send_sem, target):
        send(walkers.at[src], walkers.at[dst], send_sem, walker_recv.at[dst], target)

    def arrived(k, s):
        slot = place(k, s)
        await_copy(walkers.at[slot], walker_recv.at[slot])

    to_slot(0, place(0, 1), pair_send.at[0], partner)
    for k in range(1, depth):
        to_slot(0, place(k, 0), line_send.at[k], line[k])
    send(walkers.at[0], near_by.at[2 * core], core_send.at[0], near_recv.at[0], sibling)
    send(chol_ref, chol.at[core], core_send.at[1], chol_recv.at[0], sibling)

    lane8 = lax.broadcasted_iota(jnp.int32, (8, 128), 1)
    row8 = lax.broadcasted_iota(jnp.int32, (8, 128), 0)
    low = lax.broadcasted_iota(jnp.int32, (nocc, 128), 1) < nocc
    on_diag = (lane8 % 8) == row8
    bands = [(lane8 % nocc) // 8 == r for r in range(nocc // 8)]
    per = 128 // (2 * chol_dev)
    shift = (chip % per) * (2 * chol_dev)
    energy_row = pl.multiple_of((shift + 2 * chol_dev) % 128, 8)
    zero = jnp.zeros((8, 128), jnp.float32)
    contract = (((1,), (1,)), ((), ()))

    def compute(first, owner, sums):
        group = walkers[first : first + TILE].reshape(TILE * nocc, -1)

        def chunk(c, sums):
            at = pl.multiple_of(c * (STEP * nocc), STEP * nocc)
            part = chol[owner, pl.ds(at, STEP * nocc), :]
            forward = lax.dot_general(part, group, contract, preferred_element_type=jnp.float32)
            out = []
            for wp in range(TILE // 2):
                lanes = slice(wp * 128, wp * 128 + 128)
                total = sums[wp]
                for gp in range(STEP // 2):
                    tile = forward[gp * 128 : gp * 128 + 128, lanes]
                    mirror = tile.T
                    f0, f1 = tile[:nocc], tile[nocc:]
                    m0, m1 = mirror[:nocc], mirror[nocc:]
                    turned = pltpu.roll(jnp.where(low, m1, m0), nocc, 1)
                    product = jnp.where(low, f0, f1) * jnp.where(low, m0, m1)
                    product = product + jnp.where(low, f1, f0) * turned
                    total = total + jnp.sum(product.reshape(nocc // 8, 8, 128), axis=0)
                out.append(total)
                block = zero
                for g in range(STEP):
                    picked = forward[g * nocc : g * nocc + 8, lanes]
                    for r in range(1, nocc // 8):
                        at = g * nocc + r * 8
                        picked = jnp.where(bands[r], forward[at : at + 8, lanes], picked)
                    row = jnp.sum(jnp.where(on_diag, picked, 0.0), axis=0, keepdims=True)
                    block = jnp.where(row8 == g, row, block)
                at = pl.multiple_of(shift + owner * chol_dev + c * STEP, 8)
                diag[pl.ds(at, STEP), pl.ds(first * nocc + wp * 128, 128)] = block
            return tuple(out)

        return lax.fori_loop(0, chol_dev // STEP, chunk, sums, unroll=True)

    def finish(first, sums):
        for wp in range(TILE // 2):
            diag[pl.ds(energy_row, 8), pl.ds(first * nocc + wp * 128, 128)] = sums[wp]

    none = (zero,) * (TILE // 2)

    def forward(k):
        arrived(k, 0)
        to_slot(place(k, 0), place(k, 1), pair_send.at[k], partner)

    forward(1)
    load_chol.wait()
    arrived(0, 1)
    arrived(1, 1)
    sums = compute(0, core, none)
    for k in range(2, depth):
        forward(k)
    await_copy(chol.at[1 - core], chol_recv.at[0])
    finish(0, compute(0, 1 - core, sums))
    for first in range(TILE, half, TILE):
        for k in range(first // 2, first // 2 + TILE // 2):
            arrived(k, 1)
        finish(first, compute(first, 1 - core, compute(first, core, none)))

    table = jnp.sum(diag[...].T.reshape(half, nocc, 128), axis=1)
    for k in range(depth):
        for s in range(2):
            at = place(k, s)
            q = flip(z, k) * 2 + flip(side, s)
            message[q + 1, :, :] = table[at : at + 1, :]
    message[0, :, :] = message[half, :, :]
    message[half + 1, :, :] = message[1, :, :]

    def first_row(target):
        ahead = (target % 2 + core) % 2
        return target // 2 + 1 - ahead * (1 - target % 2)

    for k in range(1, n):
        target = (me + k) % n
        send(
            message.at[pl.ds(first_row(target), 2)],
            inbox.at[me],
            mail_send.at[k],
            mail_recv.at[me],
            target,
        )
    inbox[pl.ds(me, 1)] = message[pl.ds(chip + 1, 2)][None]

    def slot_by(q):
        k, bit = 0, 1
        while bit < depth:
            k = k + bit * ((z // bit + q // 2 // bit) % 2)
            bit *= 2
        return place(k, (side + q) % 2)

    beside = slot_by((chip + half + 1 - 2 * core) % half)
    send(walkers.at[beside], near_by.at[2 - 2 * core], core_send.at[2], near_recv.at[1], sibling)
    near_by[1] = walkers[0]
    await_copy(near_by.at[0], near_recv.at[0])
    await_copy(near_by.at[0], near_recv.at[1])

    my_count = counts_ref[me]
    slots = reloc_ref.shape[0]
    chosen = []
    for s in range(slots):
        near = lax.rem(jnp.clip(source_ref[s], 0, n - 1) - me + 1 + n, n)
        near = jnp.minimum(near, NEAR - 1)
        live = s < my_count
        value = near_by[near]
        reloc_ref[s] = jnp.where(live, value, jnp.zeros_like(value))
        chosen.append((near, live))

    for k in range(1, n):
        origin = (me + k) % n
        await_copy(inbox.at[origin], mail_recv.at[origin])

    lane1 = lax.broadcasted_iota(jnp.int32, (1, 128), 1)
    for s, (near, live) in enumerate(chosen):
        holder = jnp.where(near == 1, core, 1 - core)
        line_of = near // 2
        energy = jnp.zeros((1, 128), jnp.float32)
        for b in range(half // per):
            row = jnp.zeros((1, 128), jnp.float32)
            for q in range(per):
                got = inbox[(b * per + q) * 2 + holder, line_of]
                row = jnp.where(lane1 // (2 * chol_dev) == q, got, row)
                rest = (lane1 + (128 - (q + 1) * 2 * chol_dev)) % 128
                energy = energy + jnp.where(rest < 8, got, 0.0)
            bias_ref[s : s + 1, b * 128 : b * 128 + 128] = jnp.where(live, row, 0.0)
        energy_ref[s] = jnp.where(live, jnp.sum(energy) * (-0.5 / nchol), 0.0)

    for copy in sent:
        copy.wait_send()


def body(greens, source, counts, cholesky):
    n = lax.axis_size("walk")
    chol_dev, nocc, orbitals = cholesky.shape
    slots = source.shape[0]
    nchol = chol_dev * n
    assert greens.shape[0] == 1 and nocc == 64 and chol_dev == 32
    depth = n // 4
    half = n // 2
    return pl.pallas_call(
        functools.partial(kernel, n, nocc, chol_dev, nchol),
        out_shape=(
            pltpu.VMEM((slots, nocc, orbitals), jnp.bfloat16),
            pltpu.SMEM((slots,), jnp.float32),
            pltpu.VMEM((slots, nchol), jnp.float32),
        ),
        in_specs=[
            pl.BlockSpec(memory_space=pltpu.SMEM),
            pl.BlockSpec(memory_space=pltpu.SMEM),
            pl.BlockSpec(memory_space=pl.ANY),
            pl.BlockSpec(memory_space=pl.ANY),
        ],
        out_specs=(
            pl.BlockSpec(memory_space=pltpu.VMEM),
            pl.BlockSpec(memory_space=pltpu.SMEM),
            pl.BlockSpec(memory_space=pltpu.VMEM),
        ),
        scratch_shapes=[
            pltpu.VMEM((half, nocc, orbitals), jnp.bfloat16),
            pltpu.VMEM((2, chol_dev * nocc, orbitals), jnp.bfloat16),
            pltpu.VMEM((NEAR, nocc, orbitals), jnp.bfloat16),
            pltpu.VMEM((128, half * nocc), jnp.float32),
            pltpu.VMEM((half + 2, 1, 128), jnp.float32),
            pltpu.VMEM((n, 2, 1, 128), jnp.float32),
            pltpu.SemaphoreType.DMA((2,)),
            pltpu.SemaphoreType.DMA((depth,)),
            pltpu.SemaphoreType.DMA((depth,)),
            pltpu.SemaphoreType.DMA((3,)),
            pltpu.SemaphoreType.DMA((1,)),
            pltpu.SemaphoreType.DMA((half,)),
            pltpu.SemaphoreType.DMA((2,)),
            pltpu.SemaphoreType.DMA((n,)),
            pltpu.SemaphoreType.DMA((n,)),
        ],
        compiler_params=pltpu.CompilerParams(collective_id=0, has_side_effects=True),
    )(source, counts, greens.reshape(nocc, orbitals), cholesky.reshape(chol_dev * nocc, orbitals))


def solution(mesh):
    return jax.shard_map(
        body,
        mesh=mesh,
        in_specs=(
            P(("rep", "walk"), None, None),
            P(("rep", "walk")),
            P("rep"),
            P("walk", None, None),
        ),
        out_specs=(P(("rep", "walk"), None, None), P(("rep", "walk")), P(("rep", "walk"), None)),
        check_vma=False,
    )
```

```python
import functools

import jax
import jax.numpy as jnp
from jax import lax
from jax.experimental import pallas as pl
from jax.experimental.pallas import tpu as pltpu
from jax.sharding import PartitionSpec as P

MESH = pl.DeviceIdType.MESH
NEAR = 3
TILE = 4
STEP = 8


def kernel(
    n, nocc, chol_dev, nchol,
    source_ref, counts_ref, greens_ref, chol_ref,
    reloc_ref, energy_ref, bias_ref,
    source, counts, walkers, chol, near_by, diag, message, inbox,
    local_sem, line_ready, pair_ready,
    line_send, pair_send, core_send, chol_recv, walker_recv, near_recv, mail_send, mail_recv,
):
    me = lax.axis_index("walk")
    depth = n // 4
    half = n // 2
    core = me % 2
    side = (me // 2) % 2
    z = me // 4
    chip = me // 2

    def device_of(zz, ss, cc):
        return (zz * 2 + ss) * 2 + cc

    sibling = device_of(z, side, 1 - core)
    partner = device_of(z, 1 - side, core)
    line = [device_of(j, side, core) for j in range(depth)]

    def slot_of(j, s):
        return s * depth + j

    own = slot_of(z, side)
    def signal(sem, target):
        pl.semaphore_signal(sem, inc=1, device_id={"walk": target}, device_id_type=MESH)

    barrier = pltpu.get_barrier_semaphore()
    for j in range(1, depth):
        pl.when(j > z)(lambda: signal(barrier, line[j]))
    pl.when(side == 0)(lambda: signal(barrier, partner))
    signal(barrier, sibling)
    load_own = pltpu.make_async_copy(greens_ref, walkers.at[own], local_sem.at[0])
    load_own.start()
    pl.semaphore_wait(barrier, 1 + side + z)
    for j in range(depth - 1):
        pl.when(j < z)(lambda: signal(line_ready.at[z], line[j]))
    pl.when(side == 1)(lambda: signal(pair_ready, partner))

    load_chol = pltpu.make_async_copy(chol_ref, chol.at[core], local_sem.at[1])
    load_chol.start()
    load_source = pltpu.make_async_copy(source_ref, source, local_sem.at[2])
    load_source.start()
    load_counts = pltpu.make_async_copy(counts_ref, counts, local_sem.at[3])
    load_counts.start()
    diag[...] = jnp.zeros_like(diag)
    load_own.wait()

    sent = []

    def remote(src, dst, send_sem, recv_sem, target, when=None):
        copy = pltpu.make_async_remote_copy(
            src_ref=src,
            dst_ref=dst,
            send_sem=send_sem,
            recv_sem=recv_sem,
            device_id={"walk": target},
            device_id_type=MESH,
        )
        sent.append((copy, when))
        return copy

    def await_copy(ref, sem):
        pltpu.make_async_remote_copy(
            src_ref=ref,
            dst_ref=ref,
            send_sem=local_sem.at[0],
            recv_sem=sem,
            device_id={"walk": me},
            device_id_type=MESH,
        ).wait_recv()

    def walker_to(slot, send_sem, target, when=None):
        return remote(walkers.at[slot], walkers.at[slot], send_sem, walker_recv.at[slot], target, when)

    def arrived(slot):
        await_copy(walkers.at[slot], walker_recv.at[slot])

    to_partner = walker_to(own, pair_send.at[depth], partner)
    to_line = [walker_to(own, line_send.at[j], line[j], j != z) for j in range(depth)]
    for j in range(depth):
        walker_to(slot_of(j, side), pair_send.at[j], partner, j != z)

    for j in reversed(range(depth - 1)):
        pl.when(j < z)(to_line[j].start)
    pl.when(side == 1)(to_partner.start)

    remote(walkers.at[own], near_by.at[2 * core], core_send.at[0], near_recv.at[0], sibling).start()
    remote(chol_ref, chol.at[core], core_send.at[1], chol_recv.at[0], sibling).start()

    lane8 = lax.broadcasted_iota(jnp.int32, (8, 128), 1)
    row8 = lax.broadcasted_iota(jnp.int32, (8, 128), 0)
    low = lax.broadcasted_iota(jnp.int32, (nocc, 128), 1) < nocc
    on_diag = (lane8 % 8) == row8
    bands = [(lane8 % nocc) // 8 == r for r in range(nocc // 8)]
    per = 128 // (2 * chol_dev)
    shift = (chip % per) * (2 * chol_dev)
    energy_row = pl.multiple_of((shift + 2 * chol_dev) % 128, 8)
    zero = jnp.zeros((8, 128), jnp.float32)
    contract = (((1,), (1,)), ((), ()))

    def compute(first, owner, sums):
        group = walkers[pl.ds(first, TILE)].reshape(TILE * nocc, -1)

        def chunk(c, sums):
            at = pl.multiple_of(c * (STEP * nocc), STEP * nocc)
            part = chol[owner, pl.ds(at, STEP * nocc), :]
            rotated = lax.dot_general(part, group, contract, preferred_element_type=jnp.float32)
            out = []
            for wp in range(TILE // 2):
                lanes = slice(wp * 128, wp * 128 + 128)
                total = sums[wp]
                for gp in range(STEP // 2):
                    tile = rotated[gp * 128 : gp * 128 + 128, lanes]
                    mirror = tile.T
                    f0, f1 = tile[:nocc], tile[nocc:]
                    m0, m1 = mirror[:nocc], mirror[nocc:]
                    turned = pltpu.roll(jnp.where(low, m1, m0), nocc, 1)
                    product = jnp.where(low, f0, f1) * jnp.where(low, m0, m1)
                    product = product + jnp.where(low, f1, f0) * turned
                    total = total + jnp.sum(product.reshape(nocc // 8, 8, 128), axis=0)
                out.append(total)
                block = zero
                for g in range(STEP):
                    picked = rotated[g * nocc : g * nocc + 8, lanes]
                    for r in range(1, nocc // 8):
                        at = g * nocc + r * 8
                        picked = jnp.where(bands[r], rotated[at : at + 8, lanes], picked)
                    row = jnp.sum(jnp.where(on_diag, picked, 0.0), axis=0, keepdims=True)
                    block = jnp.where(row8 == g, row, block)
                at = pl.multiple_of(shift + owner * chol_dev + c * STEP, 8)
                across = pl.multiple_of(first * nocc + wp * 128, 128)
                diag[pl.ds(at, STEP), pl.ds(across, 128)] = block
            return tuple(out)

        return lax.fori_loop(0, chol_dev // STEP, chunk, sums, unroll=True)

    def close(first, sums):
        for wp in range(TILE // 2):
            across = pl.multiple_of(first * nocc + wp * 128, 128)
            diag[pl.ds(energy_row, 8), pl.ds(across, 128)] = sums[wp]

    none = (zero,) * (TILE // 2)

    @pl.when(side == 0)
    def _():
        pl.semaphore_wait(pair_ready, 1)
        to_partner.start()

    for j in range(depth):

        @pl.when(j > z)
        def _():
            pl.semaphore_wait(line_ready.at[j], 1)
            to_line[j].start()

    for away in range(1, depth):
        for j in (z - away, z + away):

            @pl.when((j >= 0) & (j < depth))
            def _():
                slot = slot_of(j, side)
                arrived(slot)
                walker_to(slot, pair_send.at[j], partner).start()
                sent.pop()

    def tabulate(s):
        lanes = diag[:, pl.ds(pl.multiple_of(s * depth * nocc, 128), depth * nocc)]
        table = jnp.sum(lanes.T.reshape(depth, nocc, 128), axis=1)
        for j in range(depth):
            message[2 * j + s + 1, :, :] = table[j : j + 1, :]

    load_chol.wait()
    for step in range(depth // TILE):
        first = side * depth + step * TILE
        sums = compute(first, core, none)
        if step == 0:
            await_copy(chol.at[1 - core], chol_recv.at[0])
        close(first, compute(first, 1 - core, sums))
    tabulate(side)

    for step in range(depth // TILE):
        for j in range(step * TILE, step * TILE + TILE):
            arrived(slot_of(j, 1 - side))
        if step == depth // TILE - 1:
            beside = (chip + half + 1 - 2 * core) % half
            remote(
                walkers.at[slot_of(beside // 2, 1 - side)],
                near_by.at[2 - 2 * core],
                core_send.at[2],
                near_recv.at[1],
                sibling,
            ).start()
        first = (1 - side) * depth + step * TILE
        close(first, compute(first, 1 - core, compute(first, core, none)))
    tabulate(1 - side)
    message[0, :, :] = message[half, :, :]
    message[half + 1, :, :] = message[1, :, :]

    for k in range(1, n):
        target = (me + k) % n
        behind = (target + core) % 2
        row = target // 2 + 1 - behind * (1 - target % 2)
        remote(
            message.at[pl.ds(row, 2)], inbox.at[me], mail_send.at[k], mail_recv.at[me], target
        ).start()
    inbox[pl.ds(me, 1)] = message[pl.ds(chip + 1, 2)][None]

    near_by[1] = walkers[own]
    await_copy(near_by.at[0], near_recv.at[0])
    await_copy(near_by.at[0], near_recv.at[1])

    load_source.wait()
    load_counts.wait()
    my_count = counts[me]
    slots = reloc_ref.shape[0]
    chosen = []
    for s in range(slots):
        near = lax.rem(jnp.clip(source[s], 0, n - 1) - me + 1 + n, n)
        near = jnp.minimum(near, NEAR - 1)
        live = s < my_count
        value = near_by[near]
        reloc_ref[s] = jnp.where(live, value, jnp.zeros_like(value))
        chosen.append((near, live))

    for k in range(1, n):
        origin = (me + k) % n
        await_copy(inbox.at[origin], mail_recv.at[origin])

    lane1 = lax.broadcasted_iota(jnp.int32, (1, 128), 1)
    for s, (near, live) in enumerate(chosen):
        holder = jnp.where(near == 1, core, 1 - core)
        row_of = near // 2
        energy = jnp.zeros((1, 128), jnp.float32)
        for b in range(half // per):
            row = jnp.zeros((1, 128), jnp.float32)
            for q in range(per):
                got = inbox[(b * per + q) * 2 + holder, row_of]
                row = jnp.where(lane1 // (2 * chol_dev) == q, got, row)
                rest = (lane1 + (128 - (q + 1) * 2 * chol_dev)) % 128
                energy = energy + jnp.where(rest < 8, got, 0.0)
            bias_ref[s : s + 1, b * 128 : b * 128 + 128] = jnp.where(live, row, 0.0)
        energy_ref[s] = jnp.where(live, jnp.sum(energy) * (-0.5 / nchol), 0.0)

    for copy, when in sent:
        if when is None:
            copy.wait_send()
        else:
            pl.when(when)(copy.wait_send)


def store(reloc_ref, energy_ref, bias_ref, reloc_out, energy_out, bias_out, sems):
    pairs = ((reloc_ref, reloc_out), (energy_ref, energy_out), (bias_ref, bias_out))
    copies = [pltpu.make_async_copy(src, dst, sems.at[i]) for i, (src, dst) in enumerate(pairs)]
    for copy in copies:
        copy.start()
    for copy in copies:
        copy.wait()


def body(greens, source, counts, cholesky):
    n = lax.axis_size("walk")
    chol_dev, nocc, orbitals = cholesky.shape
    slots = source.shape[0]
    nchol = chol_dev * n
    assert greens.shape[0] == 1 and nocc == 64 and chol_dev == 32
    depth = n // 4
    half = n // 2
    results = pl.pallas_call(
        functools.partial(kernel, n, nocc, chol_dev, nchol),
        out_shape=(
            pltpu.VMEM((slots, nocc, orbitals), jnp.bfloat16),
            pltpu.SMEM((slots,), jnp.float32),
            pltpu.VMEM((slots, nchol), jnp.float32),
        ),
        in_specs=[
            pl.BlockSpec(memory_space=pl.ANY),
            pl.BlockSpec(memory_space=pl.ANY),
            pl.BlockSpec(memory_space=pl.ANY),
            pl.BlockSpec(memory_space=pl.ANY),
        ],
        out_specs=(
            pl.BlockSpec(memory_space=pltpu.VMEM),
            pl.BlockSpec(memory_space=pltpu.SMEM),
            pl.BlockSpec(memory_space=pltpu.VMEM),
        ),
        scratch_shapes=[
            pltpu.SMEM((slots,), jnp.int32),
            pltpu.SMEM(counts.shape, jnp.int32),
            pltpu.VMEM((half, nocc, orbitals), jnp.bfloat16),
            pltpu.VMEM((2, chol_dev * nocc, orbitals), jnp.bfloat16),
            pltpu.VMEM((NEAR, nocc, orbitals), jnp.bfloat16),
            pltpu.VMEM((128, half * nocc), jnp.float32),
            pltpu.VMEM((half + 2, 1, 128), jnp.float32),
            pltpu.VMEM((n, 2, 1, 128), jnp.float32),
            pltpu.SemaphoreType.DMA((4,)),
            pltpu.SemaphoreType.REGULAR((depth,)),
            pltpu.SemaphoreType.REGULAR,
            pltpu.SemaphoreType.DMA((depth,)),
            pltpu.SemaphoreType.DMA((depth + 1,)),
            pltpu.SemaphoreType.DMA((3,)),
            pltpu.SemaphoreType.DMA((1,)),
            pltpu.SemaphoreType.DMA((half,)),
            pltpu.SemaphoreType.DMA((2,)),
            pltpu.SemaphoreType.DMA((n,)),
            pltpu.SemaphoreType.DMA((n,)),
        ],
        compiler_params=pltpu.CompilerParams(collective_id=0, has_side_effects=True),
    )(source, counts, greens.reshape(nocc, orbitals), cholesky.reshape(chol_dev * nocc, orbitals))
    places = (pltpu.VMEM, pltpu.SMEM, pltpu.VMEM)
    return pl.pallas_call(
        store,
        out_shape=tuple(jax.ShapeDtypeStruct(x.shape, x.dtype) for x in results),
        in_specs=[pl.BlockSpec(memory_space=m) for m in places],
        out_specs=(pl.BlockSpec(memory_space=pl.ANY),) * 3,
        scratch_shapes=[pltpu.SemaphoreType.DMA((3,))],
    )(*[pltpu.with_memory_space_constraint(x, m) for x, m in zip(results, places)])


def solution(mesh):
    return jax.shard_map(
        body,
        mesh=mesh,
        in_specs=(
            P(("rep", "walk"), None, None),
            P(("rep", "walk")),
            P("rep"),
            P("walk", None, None),
        ),
        out_specs=(P(("rep", "walk"), None, None), P(("rep", "walk")), P(("rep", "walk"), None)),
        check_vma=False,
    )
```

```python
import functools

import jax
import jax.numpy as jnp
from jax import lax
from jax.experimental import pallas as pl
from jax.experimental.pallas import tpu as pltpu
from jax.sharding import PartitionSpec as P

MESH = pl.DeviceIdType.MESH
NEAR = 3
TILE = 4
STEP = 8
LAST = 0


def kernel(
    n, nocc, chol_dev, nchol,
    source_ref, counts_ref, greens_ref, chol_ref,
    reloc_ref, energy_ref, bias_ref,
    source, counts, walkers, chol, near_by, diag, message, inbox,
    local_sem, line_ready, pair_ready,
    line_send, pair_send, core_send, chol_recv, walker_recv, near_recv, mail_send, mail_recv,
):
    me = lax.axis_index("walk")
    depth = n // 4
    half = n // 2
    core = me % 2
    side = (me // 2) % 2
    z = me // 4
    chip = me // 2

    def device_of(zz, ss, cc):
        return (zz * 2 + ss) * 2 + cc

    sibling = device_of(z, side, 1 - core)
    partner = device_of(z, 1 - side, core)
    line = [device_of(j, side, core) for j in range(depth)]

    def slot_of(j, s):
        return s * depth + j

    own = slot_of(z, side)
    def signal(sem, target):
        pl.semaphore_signal(sem, inc=1, device_id={"walk": target}, device_id_type=MESH)

    barrier = pltpu.get_barrier_semaphore()
    for j in range(1, depth):
        pl.when(j > z)(lambda: signal(barrier, line[j]))
    pl.when(side == 0)(lambda: signal(barrier, partner))
    signal(barrier, sibling)
    load_own = pltpu.make_async_copy(greens_ref, walkers.at[own], local_sem.at[0])
    load_own.start()
    pl.semaphore_wait(barrier, 1 + side + z)
    for j in range(depth - 1):
        pl.when(j < z)(lambda: signal(line_ready.at[z], line[j]))
    pl.when(side == 1)(lambda: signal(pair_ready, partner))

    load_chol = pltpu.make_async_copy(chol_ref, chol.at[core], local_sem.at[1])
    load_chol.start()
    load_source = pltpu.make_async_copy(source_ref, source, local_sem.at[2])
    load_source.start()
    load_counts = pltpu.make_async_copy(counts_ref, counts, local_sem.at[3])
    load_counts.start()
    diag[...] = jnp.zeros_like(diag)
    load_own.wait()

    sent = []

    def remote(src, dst, send_sem, recv_sem, target, when=None):
        copy = pltpu.make_async_remote_copy(
            src_ref=src,
            dst_ref=dst,
            send_sem=send_sem,
            recv_sem=recv_sem,
            device_id={"walk": target},
            device_id_type=MESH,
        )
        sent.append((copy, when))
        return copy

    def await_copy(ref, sem):
        pltpu.make_async_remote_copy(
            src_ref=ref,
            dst_ref=ref,
            send_sem=local_sem.at[0],
            recv_sem=sem,
            device_id={"walk": me},
            device_id_type=MESH,
        ).wait_recv()

    def walker_to(slot, send_sem, target, when=None):
        return remote(walkers.at[slot], walkers.at[slot], send_sem, walker_recv.at[slot], target, when)

    def arrived(slot):
        await_copy(walkers.at[slot], walker_recv.at[slot])

    to_partner = walker_to(own, pair_send.at[depth], partner)
    to_line = [walker_to(own, line_send.at[j], line[j], j != z) for j in range(depth)]
    for j in range(depth):
        walker_to(slot_of(j, side), pair_send.at[j], partner, j != z)

    for j in reversed(range(depth - 1)):
        pl.when(j < z)(to_line[j].start)
    pl.when(side == 1)(to_partner.start)

    remote(walkers.at[own], near_by.at[2 * core], core_send.at[0], near_recv.at[0], sibling).start()
    remote(chol_ref, chol.at[core], core_send.at[1], chol_recv.at[0], sibling).start()

    lane8 = lax.broadcasted_iota(jnp.int32, (8, 128), 1)
    row8 = lax.broadcasted_iota(jnp.int32, (8, 128), 0)
    low = lax.broadcasted_iota(jnp.int32, (nocc, 128), 1) < nocc
    on_diag = (lane8 % 8) == row8
    bands = [(lane8 % nocc) // 8 == r for r in range(nocc // 8)]
    per = 128 // (2 * chol_dev)
    shift = (chip % per) * (2 * chol_dev)
    energy_row = pl.multiple_of((shift + 2 * chol_dev) % 128, 8)
    zero = jnp.zeros((8, 128), jnp.float32)
    contract = (((1,), (1,)), ((), ()))

    lane1 = lax.broadcasted_iota(jnp.int32, (1, 128), 1)
    is_energy = (lane1 >= energy_row) & (lane1 < energy_row + 8)

    def compute(slots, base, owners):
        lone = len(slots) % 2 == 1
        operands = [walkers[slot] for slot in slots] + [walkers[slots[-1]]] * lone
        group = jnp.concatenate(operands, axis=0)
        tiles = len(operands) // 2

        def chunk(owner, c, sums):
            at = pl.multiple_of(c * (STEP * nocc), STEP * nocc)
            part = chol[owner, pl.ds(at, STEP * nocc), :]
            rotated = lax.dot_general(part, group, contract, preferred_element_type=jnp.float32)
            out = []
            for t in range(tiles):
                lanes = slice(t * 128, t * 128 + 128)
                total = sums[t]
                blocks = [rotated[g * nocc : g * nocc + nocc, lanes] for g in range(STEP)]
                if lone and t == tiles - 1:
                    for f0, f1, f2, f3 in zip(*[iter(blocks)] * 4):
                        tile = jnp.concatenate([jnp.where(low, f0, f1), jnp.where(low, f2, f3)], axis=0)
                        mirror = tile.T
                        product = mirror[:nocc] * jnp.where(low, f0, f2)
                        product = product + mirror[nocc:] * jnp.where(low, f1, f3)
                        total = total + jnp.sum(product.reshape(nocc // 8, 8, 128), axis=0)
                else:
                    for f0, f1 in zip(*[iter(blocks)] * 2):
                        mirror = jnp.concatenate([f0, f1], axis=0).T
                        m0, m1 = mirror[:nocc], mirror[nocc:]
                        turned = pltpu.roll(jnp.where(low, m1, m0), nocc, 1)
                        product = jnp.where(low, f0, f1) * jnp.where(low, m0, m1)
                        product = product + jnp.where(low, f1, f0) * turned
                        total = total + jnp.sum(product.reshape(nocc // 8, 8, 128), axis=0)
                out.append(total)
                block = zero
                for g in range(STEP):
                    picked = rotated[g * nocc : g * nocc + 8, lanes]
                    for r in range(1, nocc // 8):
                        at = g * nocc + r * 8
                        picked = jnp.where(bands[r], rotated[at : at + 8, lanes], picked)
                    row = jnp.sum(jnp.where(on_diag, picked, 0.0), axis=0, keepdims=True)
                    block = jnp.where(row8 == g, row, block)
                at = pl.multiple_of(shift + owner * chol_dev + c * STEP, 8)
                diag[pl.ds(at, STEP), (base + t) * 128 : (base + t) * 128 + 128] = block
            return tuple(out)

        sums = (zero,) * tiles
        for owner in owners:
            sums = lax.fori_loop(0, chol_dev // STEP, functools.partial(chunk, owner), sums, unroll=True)
        for t in range(tiles):
            diag[pl.ds(energy_row, 8), (base + t) * 128 : (base + t) * 128 + 128] = sums[t]
        return tiles

    def tabulate(chips, base):
        tiles = (len(chips) + 1) // 2
        lanes = diag[:, base * 128 : (base + tiles) * 128]
        table = jnp.sum(lanes.T.reshape(2 * tiles, nocc, 128), axis=1)
        for t, q in enumerate(chips):
            row = table[t : t + 1, :]
            if t == len(chips) - 1 and t % 2 == 0:
                row = row + jnp.where(is_energy, table[t + 1 : t + 2, :], 0.0)
            message[q + 1, :, :] = row

    @pl.when(side == 0)
    def _():
        pl.semaphore_wait(pair_ready, 1)
        to_partner.start()

    for j in range(depth):

        @pl.when(j > z)
        def _():
            pl.semaphore_wait(line_ready.at[j], 1)
            to_line[j].start()

    owners = [core, 1 - core]
    load_chol.wait()
    await_copy(chol.at[1 - core], chol_recv.at[0])
    arrived(slot_of(z, 1 - side))
    base = compute([own, slot_of(z, 1 - side)], 0, owners)
    tabulate([chip, 2 * z + 1 - side], 0)

    room = jnp.minimum(z, depth - 1 - z)
    onward = jnp.where(z > depth - 1 - z, -1, 1)
    others = []
    for t in range(1, depth):
        near_j = z - (t + 1) // 2 if t % 2 else z + t // 2
        others.append(jnp.where(t <= 2 * room, near_j, z + onward * (t - room)))
    for j in others:
        slot = slot_of(j, side)
        arrived(slot)
        walker_to(slot, pair_send.at[j], partner).start()
        sent.pop()

    for s in (side, 1 - side):
        whole = depth - 1 - LAST * (s is not side)
        cuts = [others[at : min(at + TILE, whole)] for at in range(0, whole, TILE)] + [others[whole:]]
        for js in filter(None, cuts):
            if s is not side:
                for j in js:
                    arrived(slot_of(j, s))
                if js[-1] is others[-1]:
                    beside = (chip + half + 1 - 2 * core) % half
                    remote(
                        walkers.at[slot_of(beside // 2, 1 - side)],
                        near_by.at[2 - 2 * core],
                        core_send.at[2],
                        near_recv.at[1],
                        sibling,
                    ).start()
            tiles = compute([slot_of(j, s) for j in js], base, owners)
            tabulate([2 * j + s for j in js], base)
            base += tiles
    message[0, :, :] = message[half, :, :]
    message[half + 1, :, :] = message[1, :, :]

    moved = len(sent)
    for k in range(1, n):
        target = (me + k) % n
        behind = (target + core) % 2
        row = target // 2 + 1 - behind * (1 - target % 2)
        remote(
            message.at[pl.ds(row, 2)], inbox.at[me], mail_send.at[k], mail_recv.at[me], target
        ).start()
    inbox[pl.ds(me, 1)] = message[pl.ds(chip + 1, 2)][None]

    near_by[1] = walkers[own]
    await_copy(near_by.at[0], near_recv.at[0])
    await_copy(near_by.at[0], near_recv.at[1])

    load_source.wait()
    load_counts.wait()
    my_count = counts[me]
    slots = reloc_ref.shape[0]
    chosen = []
    for s in range(slots):
        near = lax.rem(jnp.clip(source[s], 0, n - 1) - me + 1 + n, n)
        near = jnp.minimum(near, NEAR - 1)
        live = s < my_count
        value = near_by[near]
        reloc_ref[s] = jnp.where(live, value, jnp.zeros_like(value))
        chosen.append((near, live))

    def wait_sent(copies):
        for copy, when in copies:
            if when is None:
                copy.wait_send()
            else:
                pl.when(when)(copy.wait_send)

    wait_sent(sent[:moved])
    for k in range(1, n):
        origin = (me + k) % n
        await_copy(inbox.at[origin], mail_recv.at[origin])

    for s, (near, live) in enumerate(chosen):
        holder = jnp.where(near == 1, core, 1 - core)
        row_of = near // 2
        energy = jnp.zeros((1, 128), jnp.float32)
        for b in range(half // per):
            row = jnp.zeros((1, 128), jnp.float32)
            for q in range(per):
                got = inbox[(b * per + q) * 2 + holder, row_of]
                row = jnp.where(lane1 // (2 * chol_dev) == q, got, row)
                rest = (lane1 + (128 - (q + 1) * 2 * chol_dev)) % 128
                energy = energy + jnp.where(rest < 8, got, 0.0)
            bias_ref[s : s + 1, b * 128 : b * 128 + 128] = jnp.where(live, row, 0.0)
        energy_ref[s] = jnp.where(live, jnp.sum(energy) * (-0.5 / nchol), 0.0)

    wait_sent(sent[moved:])


def store(reloc_ref, energy_ref, bias_ref, reloc_out, energy_out, bias_out, sems):
    pairs = ((reloc_ref, reloc_out), (energy_ref, energy_out), (bias_ref, bias_out))
    copies = [pltpu.make_async_copy(src, dst, sems.at[i]) for i, (src, dst) in enumerate(pairs)]
    for copy in copies:
        copy.start()
    for copy in copies:
        copy.wait()


def body(greens, source, counts, cholesky):
    n = lax.axis_size("walk")
    chol_dev, nocc, orbitals = cholesky.shape
    slots = source.shape[0]
    nchol = chol_dev * n
    assert greens.shape[0] == 1 and nocc == 64 and chol_dev == 32
    depth = n // 4
    half = n // 2
    results = pl.pallas_call(
        functools.partial(kernel, n, nocc, chol_dev, nchol),
        out_shape=(
            pltpu.VMEM((slots, nocc, orbitals), jnp.bfloat16),
            pltpu.SMEM((slots,), jnp.float32),
            pltpu.VMEM((slots, nchol), jnp.float32),
        ),
        in_specs=[
            pl.BlockSpec(memory_space=pl.ANY),
            pl.BlockSpec(memory_space=pl.ANY),
            pl.BlockSpec(memory_space=pl.ANY),
            pl.BlockSpec(memory_space=pl.ANY),
        ],
        out_specs=(
            pl.BlockSpec(memory_space=pltpu.VMEM),
            pl.BlockSpec(memory_space=pltpu.SMEM),
            pl.BlockSpec(memory_space=pltpu.VMEM),
        ),
        scratch_shapes=[
            pltpu.SMEM((slots,), jnp.int32),
            pltpu.SMEM(counts.shape, jnp.int32),
            pltpu.VMEM((half, nocc, orbitals), jnp.bfloat16),
            pltpu.VMEM((2, chol_dev * nocc, orbitals), jnp.bfloat16),
            pltpu.VMEM((NEAR, nocc, orbitals), jnp.bfloat16),
            pltpu.VMEM((128, (2 + 2 * (depth // 2)) * 128), jnp.float32),
            pltpu.VMEM((half + 2, 1, 128), jnp.float32),
            pltpu.VMEM((n, 2, 1, 128), jnp.float32),
            pltpu.SemaphoreType.DMA((4,)),
            pltpu.SemaphoreType.REGULAR((depth,)),
            pltpu.SemaphoreType.REGULAR,
            pltpu.SemaphoreType.DMA((depth,)),
            pltpu.SemaphoreType.DMA((depth + 1,)),
            pltpu.SemaphoreType.DMA((3,)),
            pltpu.SemaphoreType.DMA((1,)),
            pltpu.SemaphoreType.DMA((half,)),
            pltpu.SemaphoreType.DMA((2,)),
            pltpu.SemaphoreType.DMA((n,)),
            pltpu.SemaphoreType.DMA((n,)),
        ],
        compiler_params=pltpu.CompilerParams(collective_id=0, has_side_effects=True),
    )(source, counts, greens.reshape(nocc, orbitals), cholesky.reshape(chol_dev * nocc, orbitals))
    places = (pltpu.VMEM, pltpu.SMEM, pltpu.VMEM)
    return pl.pallas_call(
        store,
        out_shape=tuple(jax.ShapeDtypeStruct(x.shape, x.dtype) for x in results),
        in_specs=[pl.BlockSpec(memory_space=m) for m in places],
        out_specs=(pl.BlockSpec(memory_space=pl.ANY),) * 3,
        scratch_shapes=[pltpu.SemaphoreType.DMA((3,))],
    )(*[pltpu.with_memory_space_constraint(x, m) for x, m in zip(results, places)])


def solution(mesh):
    return jax.shard_map(
        body,
        mesh=mesh,
        in_specs=(
            P(("rep", "walk"), None, None),
            P(("rep", "walk")),
            P("rep"),
            P("walk", None, None),
        ),
        out_specs=(P(("rep", "walk"), None, None), P(("rep", "walk")), P(("rep", "walk"), None)),
        check_vma=False,
    )
```

```python
import functools

import jax
import jax.numpy as jnp
from jax import lax
from jax.experimental import pallas as pl
from jax.experimental.pallas import tpu as pltpu
from jax.sharding import PartitionSpec as P

MESH = pl.DeviceIdType.MESH
NEAR = 3
TILE = 4
STEP = 8
LAST = 2


def kernel(
    n, nocc, chol_dev, nchol,
    source_ref, counts_ref, greens_ref, chol_ref,
    reloc_ref, energy_ref, bias_ref,
    source, counts, walkers, chol, near_by, diag, message, inbox,
    local_sem, line_ready, pair_ready,
    line_send, pair_send, core_send, chol_recv, walker_recv, near_recv, mail_send, mail_recv,
):
    me = lax.axis_index("walk")
    depth = n // 4
    half = n // 2
    core = me % 2
    side = (me // 2) % 2
    z = me // 4
    chip = me // 2

    def device_of(zz, ss, cc):
        return (zz * 2 + ss) * 2 + cc

    sibling = device_of(z, side, 1 - core)
    partner = device_of(z, 1 - side, core)
    line = [device_of(j, side, core) for j in range(depth)]

    def slot_of(j, s):
        return s * depth + j

    own = slot_of(z, side)
    def signal(sem, target):
        pl.semaphore_signal(sem, inc=1, device_id={"walk": target}, device_id_type=MESH)

    barrier = pltpu.get_barrier_semaphore()
    for j in range(1, depth):
        pl.when(j > z)(lambda: signal(barrier, line[j]))
    pl.when(side == 0)(lambda: signal(barrier, partner))
    signal(barrier, sibling)
    load_own = pltpu.make_async_copy(greens_ref, walkers.at[own], local_sem.at[0])
    load_own.start()
    pl.semaphore_wait(barrier, 1 + side + z)
    for j in range(depth - 1):
        pl.when(j < z)(lambda: signal(line_ready.at[z], line[j]))
    pl.when(side == 1)(lambda: signal(pair_ready, partner))

    load_chol = pltpu.make_async_copy(chol_ref, chol.at[core], local_sem.at[1])
    load_chol.start()
    load_source = pltpu.make_async_copy(source_ref, source, local_sem.at[2])
    load_source.start()
    load_counts = pltpu.make_async_copy(counts_ref, counts, local_sem.at[3])
    load_counts.start()
    diag[...] = jnp.zeros_like(diag)
    load_own.wait()

    sent = []

    def remote(src, dst, send_sem, recv_sem, target, when=None):
        copy = pltpu.make_async_remote_copy(
            src_ref=src,
            dst_ref=dst,
            send_sem=send_sem,
            recv_sem=recv_sem,
            device_id={"walk": target},
            device_id_type=MESH,
        )
        sent.append((copy, when))
        return copy

    def await_copy(ref, sem):
        pltpu.make_async_remote_copy(
            src_ref=ref,
            dst_ref=ref,
            send_sem=local_sem.at[0],
            recv_sem=sem,
            device_id={"walk": me},
            device_id_type=MESH,
        ).wait_recv()

    def walker_to(slot, send_sem, target, when=None):
        return remote(walkers.at[slot], walkers.at[slot], send_sem, walker_recv.at[slot], target, when)

    def arrived(slot):
        await_copy(walkers.at[slot], walker_recv.at[slot])

    to_partner = walker_to(own, pair_send.at[depth], partner)
    to_line = [walker_to(own, line_send.at[j], line[j], j != z) for j in range(depth)]
    for j in range(depth):
        walker_to(slot_of(j, side), pair_send.at[j], partner, j != z)

    for j in reversed(range(depth - 1)):
        pl.when(j < z)(to_line[j].start)
    pl.when(side == 1)(to_partner.start)

    remote(walkers.at[own], near_by.at[2 * core], core_send.at[0], near_recv.at[0], sibling).start()
    remote(chol_ref, chol.at[core], core_send.at[1], chol_recv.at[0], sibling).start()

    lane8 = lax.broadcasted_iota(jnp.int32, (8, 128), 1)
    row8 = lax.broadcasted_iota(jnp.int32, (8, 128), 0)
    low = lax.broadcasted_iota(jnp.int32, (nocc, 128), 1) < nocc
    on_diag = (lane8 % 8) == row8
    bands = [(lane8 % nocc) // 8 == r for r in range(nocc // 8)]
    per = 128 // (2 * chol_dev)
    shift = (chip % per) * (2 * chol_dev)
    energy_row = pl.multiple_of((shift + 2 * chol_dev) % 128, 8)
    zero = jnp.zeros((8, 128), jnp.float32)
    contract = (((1,), (1,)), ((), ()))

    lane1 = lax.broadcasted_iota(jnp.int32, (1, 128), 1)
    is_energy = (lane1 >= energy_row) & (lane1 < energy_row + 8)

    def compute(slots, base, owners):
        lone = len(slots) % 2 == 1
        operands = [walkers[slot] for slot in slots] + [walkers[slots[-1]]] * lone
        group = jnp.concatenate(operands, axis=0)
        tiles = len(operands) // 2

        def chunk(owner, c, sums):
            at = pl.multiple_of(c * (STEP * nocc), STEP * nocc)
            part = chol[owner, pl.ds(at, STEP * nocc), :]
            rotated = lax.dot_general(part, group, contract, preferred_element_type=jnp.float32)
            out = []
            for t in range(tiles):
                lanes = slice(t * 128, t * 128 + 128)
                total = sums[t]
                blocks = [rotated[g * nocc : g * nocc + nocc, lanes] for g in range(STEP)]
                if lone and t == tiles - 1:
                    for f0, f1, f2, f3 in zip(*[iter(blocks)] * 4):
                        tile = jnp.concatenate([jnp.where(low, f0, f1), jnp.where(low, f2, f3)], axis=0)
                        mirror = tile.T
                        product = mirror[:nocc] * jnp.where(low, f0, f2)
                        product = product + mirror[nocc:] * jnp.where(low, f1, f3)
                        total = total + jnp.sum(product.reshape(nocc // 8, 8, 128), axis=0)
                else:
                    for f0, f1 in zip(*[iter(blocks)] * 2):
                        mirror = jnp.concatenate([f0, f1], axis=0).T
                        m0, m1 = mirror[:nocc], mirror[nocc:]
                        turned = pltpu.roll(jnp.where(low, m1, m0), nocc, 1)
                        product = jnp.where(low, f0, f1) * jnp.where(low, m0, m1)
                        product = product + jnp.where(low, f1, f0) * turned
                        total = total + jnp.sum(product.reshape(nocc // 8, 8, 128), axis=0)
                out.append(total)
                block = zero
                for g in range(STEP):
                    picked = rotated[g * nocc : g * nocc + 8, lanes]
                    for r in range(1, nocc // 8):
                        at = g * nocc + r * 8
                        picked = jnp.where(bands[r], rotated[at : at + 8, lanes], picked)
                    row = jnp.sum(jnp.where(on_diag, picked, 0.0), axis=0, keepdims=True)
                    block = jnp.where(row8 == g, row, block)
                at = pl.multiple_of(shift + owner * chol_dev + c * STEP, 8)
                diag[pl.ds(at, STEP), (base + t) * 128 : (base + t) * 128 + 128] = block
            return tuple(out)

        sums = (zero,) * tiles
        for owner in owners:
            sums = lax.fori_loop(0, chol_dev // STEP, functools.partial(chunk, owner), sums, unroll=True)
        for t in range(tiles):
            diag[pl.ds(energy_row, 8), (base + t) * 128 : (base + t) * 128 + 128] = sums[t]
        return tiles

    def tabulate(chips, base):
        tiles = (len(chips) + 1) // 2
        lanes = diag[:, base * 128 : (base + tiles) * 128]
        table = jnp.sum(lanes.T.reshape(2 * tiles, nocc, 128), axis=1)
        for t, q in enumerate(chips):
            row = table[t : t + 1, :]
            if t == len(chips) - 1 and t % 2 == 0:
                row = row + jnp.where(is_energy, table[t + 1 : t + 2, :], 0.0)
            message[q + 1, :, :] = row

    @pl.when(side == 0)
    def _():
        pl.semaphore_wait(pair_ready, 1)
        to_partner.start()

    for j in range(depth):

        @pl.when(j > z)
        def _():
            pl.semaphore_wait(line_ready.at[j], 1)
            to_line[j].start()

    owners = [core, 1 - core]
    load_chol.wait()
    await_copy(chol.at[1 - core], chol_recv.at[0])
    arrived(slot_of(z, 1 - side))
    base = compute([own, slot_of(z, 1 - side)], 0, owners)
    tabulate([chip, 2 * z + 1 - side], 0)

    room = jnp.minimum(z, depth - 1 - z)
    onward = jnp.where(z > depth - 1 - z, -1, 1)
    others = []
    for t in range(1, depth):
        near_j = z - (t + 1) // 2 if t % 2 else z + t // 2
        others.append(jnp.where(t <= 2 * room, near_j, z + onward * (t - room)))
    for j in others:
        slot = slot_of(j, side)
        arrived(slot)
        walker_to(slot, pair_send.at[j], partner).start()
        sent.pop()

    for s in (side, 1 - side):
        whole = depth - 1 - LAST * (s is not side)
        cuts = [others[at : min(at + TILE, whole)] for at in range(0, whole, TILE)] + [others[whole:]]
        for js in filter(None, cuts):
            if s is not side:
                for j in js:
                    arrived(slot_of(j, s))
                if js[-1] is others[-1]:
                    beside = (chip + half + 1 - 2 * core) % half
                    remote(
                        walkers.at[slot_of(beside // 2, 1 - side)],
                        near_by.at[2 - 2 * core],
                        core_send.at[2],
                        near_recv.at[1],
                        sibling,
                    ).start()
            tiles = compute([slot_of(j, s) for j in js], base, owners)
            tabulate([2 * j + s for j in js], base)
            base += tiles
    message[0, :, :] = message[half, :, :]
    message[half + 1, :, :] = message[1, :, :]

    moved = len(sent)
    for k in range(1, n):
        target = (me + k) % n
        behind = (target + core) % 2
        row = target // 2 + 1 - behind * (1 - target % 2)
        remote(
            message.at[pl.ds(row, 2)], inbox.at[me], mail_send.at[k], mail_recv.at[me], target
        ).start()
    inbox[pl.ds(me, 1)] = message[pl.ds(chip + 1, 2)][None]

    near_by[1] = walkers[own]
    await_copy(near_by.at[0], near_recv.at[0])
    await_copy(near_by.at[0], near_recv.at[1])

    load_source.wait()
    load_counts.wait()
    my_count = counts[me]
    slots = reloc_ref.shape[0]
    chosen = []
    for s in range(slots):
        near = lax.rem(jnp.clip(source[s], 0, n - 1) - me + 1 + n, n)
        near = jnp.minimum(near, NEAR - 1)
        live = s < my_count
        value = near_by[near]
        reloc_ref[s] = jnp.where(live, value, jnp.zeros_like(value))
        chosen.append((near, live))

    def wait_sent(copies):
        for copy, when in copies:
            if when is None:
                copy.wait_send()
            else:
                pl.when(when)(copy.wait_send)

    wait_sent(sent[:moved])
    for k in range(1, n):
        origin = (me + k) % n
        await_copy(inbox.at[origin], mail_recv.at[origin])

    for s, (near, live) in enumerate(chosen):
        holder = jnp.where(near == 1, core, 1 - core)
        row_of = near // 2
        energy = jnp.zeros((1, 128), jnp.float32)
        for b in range(half // per):
            row = jnp.zeros((1, 128), jnp.float32)
            for q in range(per):
                got = inbox[(b * per + q) * 2 + holder, row_of]
                row = jnp.where(lane1 // (2 * chol_dev) == q, got, row)
                rest = (lane1 + (128 - (q + 1) * 2 * chol_dev)) % 128
                energy = energy + jnp.where(rest < 8, got, 0.0)
            bias_ref[s : s + 1, b * 128 : b * 128 + 128] = jnp.where(live, row, 0.0)
        energy_ref[s] = jnp.where(live, jnp.sum(energy) * (-0.5 / nchol), 0.0)

    wait_sent(sent[moved:])


def store(reloc_ref, energy_ref, bias_ref, reloc_out, energy_out, bias_out, sems):
    pairs = ((reloc_ref, reloc_out), (energy_ref, energy_out), (bias_ref, bias_out))
    copies = [pltpu.make_async_copy(src, dst, sems.at[i]) for i, (src, dst) in enumerate(pairs)]
    for copy in copies:
        copy.start()
    for copy in copies:
        copy.wait()


def body(greens, source, counts, cholesky):
    n = lax.axis_size("walk")
    chol_dev, nocc, orbitals = cholesky.shape
    slots = source.shape[0]
    nchol = chol_dev * n
    assert greens.shape[0] == 1 and nocc == 64 and chol_dev == 32
    depth = n // 4
    half = n // 2
    results = pl.pallas_call(
        functools.partial(kernel, n, nocc, chol_dev, nchol),
        out_shape=(
            pltpu.VMEM((slots, nocc, orbitals), jnp.bfloat16),
            pltpu.SMEM((slots,), jnp.float32),
            pltpu.VMEM((slots, nchol), jnp.float32),
        ),
        in_specs=[
            pl.BlockSpec(memory_space=pl.ANY),
            pl.BlockSpec(memory_space=pl.ANY),
            pl.BlockSpec(memory_space=pl.ANY),
            pl.BlockSpec(memory_space=pl.ANY),
        ],
        out_specs=(
            pl.BlockSpec(memory_space=pltpu.VMEM),
            pl.BlockSpec(memory_space=pltpu.SMEM),
            pl.BlockSpec(memory_space=pltpu.VMEM),
        ),
        scratch_shapes=[
            pltpu.SMEM((slots,), jnp.int32),
            pltpu.SMEM(counts.shape, jnp.int32),
            pltpu.VMEM((half, nocc, orbitals), jnp.bfloat16),
            pltpu.VMEM((2, chol_dev * nocc, orbitals), jnp.bfloat16),
            pltpu.VMEM((NEAR, nocc, orbitals), jnp.bfloat16),
            pltpu.VMEM((128, (2 + 2 * (depth // 2)) * 128), jnp.float32),
            pltpu.VMEM((half + 2, 1, 128), jnp.float32),
            pltpu.VMEM((n, 2, 1, 128), jnp.float32),
            pltpu.SemaphoreType.DMA((4,)),
            pltpu.SemaphoreType.REGULAR((depth,)),
            pltpu.SemaphoreType.REGULAR,
            pltpu.SemaphoreType.DMA((depth,)),
            pltpu.SemaphoreType.DMA((depth + 1,)),
            pltpu.SemaphoreType.DMA((3,)),
            pltpu.SemaphoreType.DMA((1,)),
            pltpu.SemaphoreType.DMA((half,)),
            pltpu.SemaphoreType.DMA((2,)),
            pltpu.SemaphoreType.DMA((n,)),
            pltpu.SemaphoreType.DMA((n,)),
        ],
        compiler_params=pltpu.CompilerParams(collective_id=0, has_side_effects=True),
    )(source, counts, greens.reshape(nocc, orbitals), cholesky.reshape(chol_dev * nocc, orbitals))
    places = (pltpu.VMEM, pltpu.SMEM, pltpu.VMEM)
    return pl.pallas_call(
        store,
        out_shape=tuple(jax.ShapeDtypeStruct(x.shape, x.dtype) for x in results),
        in_specs=[pl.BlockSpec(memory_space=m) for m in places],
        out_specs=(pl.BlockSpec(memory_space=pl.ANY),) * 3,
        scratch_shapes=[pltpu.SemaphoreType.DMA((3,))],
    )(*[pltpu.with_memory_space_constraint(x, m) for x, m in zip(results, places)])


def solution(mesh):
    return jax.shard_map(
        body,
        mesh=mesh,
        in_specs=(
            P(("rep", "walk"), None, None),
            P(("rep", "walk")),
            P("rep"),
            P("walk", None, None),
        ),
        out_specs=(P(("rep", "walk"), None, None), P(("rep", "walk")), P(("rep", "walk"), None)),
        check_vma=False,
    )
```

```python
import functools

import jax
import jax.numpy as jnp
from jax import lax
from jax.experimental import pallas as pl
from jax.experimental.pallas import tpu as pltpu
from jax.sharding import PartitionSpec as P

MESH = pl.DeviceIdType.MESH
NEAR = 3
TILE = 4
STEP = 8
LAST = 2


def kernel(
    n, nocc, chol_dev, nchol,
    source_ref, counts_ref, greens_ref, chol_ref,
    reloc_ref, energy_ref, bias_ref,
    source, counts, walkers, chol, near_by, diag, message, inbox,
    local_sem, line_ready, pair_ready,
    line_send, pair_send, core_send, chol_recv, walker_recv, near_recv, mail_send, mail_recv,
):
    me = lax.axis_index("walk")
    depth = n // 4
    half = n // 2
    core = me % 2
    side = (me // 2) % 2
    z = me // 4
    chip = me // 2

    def device_of(zz, ss, cc):
        return (zz * 2 + ss) * 2 + cc

    sibling = device_of(z, side, 1 - core)
    partner = device_of(z, 1 - side, core)
    line = [device_of(j, side, core) for j in range(depth)]

    def slot_of(j, s):
        return s * depth + j

    own = slot_of(z, side)
    def signal(sem, target):
        pl.semaphore_signal(sem, inc=1, device_id={"walk": target}, device_id_type=MESH)

    barrier = pltpu.get_barrier_semaphore()
    for j in range(1, depth):
        pl.when(j > z)(lambda: signal(barrier, line[j]))
    pl.when(side == 0)(lambda: signal(barrier, partner))
    signal(barrier, sibling)
    load_own = pltpu.make_async_copy(greens_ref, walkers.at[own], local_sem.at[0])
    load_own.start()
    pl.semaphore_wait(barrier, 1 + side + z)
    for j in range(depth - 1):
        pl.when(j < z)(lambda: signal(line_ready.at[z], line[j]))
    pl.when(side == 1)(lambda: signal(pair_ready, partner))

    load_chol = pltpu.make_async_copy(chol_ref, chol.at[core], local_sem.at[1])
    load_chol.start()
    load_source = pltpu.make_async_copy(source_ref, source, local_sem.at[2])
    load_source.start()
    load_counts = pltpu.make_async_copy(counts_ref, counts, local_sem.at[3])
    load_counts.start()
    diag[...] = jnp.zeros_like(diag)
    load_own.wait()

    sent = []

    def remote(src, dst, send_sem, recv_sem, target, when=None):
        copy = pltpu.make_async_remote_copy(
            src_ref=src,
            dst_ref=dst,
            send_sem=send_sem,
            recv_sem=recv_sem,
            device_id={"walk": target},
            device_id_type=MESH,
        )
        sent.append((copy, when))
        return copy

    def await_copy(ref, sem):
        pltpu.make_async_remote_copy(
            src_ref=ref,
            dst_ref=ref,
            send_sem=local_sem.at[0],
            recv_sem=sem,
            device_id={"walk": me},
            device_id_type=MESH,
        ).wait_recv()

    def walker_to(slot, send_sem, target, when=None):
        return remote(walkers.at[slot], walkers.at[slot], send_sem, walker_recv.at[slot], target, when)

    def arrived(slot):
        await_copy(walkers.at[slot], walker_recv.at[slot])

    to_partner = walker_to(own, pair_send.at[depth], partner)
    to_line = [walker_to(own, line_send.at[j], line[j], j != z) for j in range(depth)]
    for j in range(depth):
        walker_to(slot_of(j, side), pair_send.at[j], partner, j != z)

    pl.when(side == 1)(to_partner.start)
    for j in range(depth - 1):
        pl.when(j < z)(to_line[j].start)

    remote(walkers.at[own], near_by.at[2 * core], core_send.at[0], near_recv.at[0], sibling).start()
    remote(chol_ref, chol.at[core], core_send.at[1], chol_recv.at[0], sibling).start()

    lane8 = lax.broadcasted_iota(jnp.int32, (8, 128), 1)
    row8 = lax.broadcasted_iota(jnp.int32, (8, 128), 0)
    low = lax.broadcasted_iota(jnp.int32, (nocc, 128), 1) < nocc
    on_diag = (lane8 % 8) == row8
    bands = [(lane8 % nocc) // 8 == r for r in range(nocc // 8)]
    per = 128 // (2 * chol_dev)
    shift = (chip % per) * (2 * chol_dev)
    energy_row = pl.multiple_of((shift + 2 * chol_dev) % 128, 8)
    zero = jnp.zeros((8, 128), jnp.float32)
    contract = (((1,), (1,)), ((), ()))

    lane1 = lax.broadcasted_iota(jnp.int32, (1, 128), 1)
    is_energy = (lane1 >= energy_row) & (lane1 < energy_row + 8)

    def compute(slots, base, owners):
        lone = len(slots) % 2 == 1
        operands = [walkers[slot] for slot in slots] + [walkers[slots[-1]]] * lone
        group = jnp.concatenate(operands, axis=0)
        tiles = len(operands) // 2

        def chunk(owner, c, sums):
            at = pl.multiple_of(c * (STEP * nocc), STEP * nocc)
            part = chol[owner, pl.ds(at, STEP * nocc), :]
            rotated = lax.dot_general(part, group, contract, preferred_element_type=jnp.float32)
            out = []
            for t in range(tiles):
                lanes = slice(t * 128, t * 128 + 128)
                total = sums[t]
                blocks = [rotated[g * nocc : g * nocc + nocc, lanes] for g in range(STEP)]
                if lone and t == tiles - 1:
                    for f0, f1, f2, f3 in zip(*[iter(blocks)] * 4):
                        tile = jnp.concatenate([jnp.where(low, f0, f1), jnp.where(low, f2, f3)], axis=0)
                        mirror = tile.T
                        product = mirror[:nocc] * jnp.where(low, f0, f2)
                        product = product + mirror[nocc:] * jnp.where(low, f1, f3)
                        total = total + jnp.sum(product.reshape(nocc // 8, 8, 128), axis=0)
                else:
                    for f0, f1 in zip(*[iter(blocks)] * 2):
                        mirror = jnp.concatenate([f0, f1], axis=0).T
                        m0, m1 = mirror[:nocc], mirror[nocc:]
                        turned = pltpu.roll(jnp.where(low, m1, m0), nocc, 1)
                        product = jnp.where(low, f0, f1) * jnp.where(low, m0, m1)
                        product = product + jnp.where(low, f1, f0) * turned
                        total = total + jnp.sum(product.reshape(nocc // 8, 8, 128), axis=0)
                out.append(total)
                block = zero
                for g in range(STEP):
                    picked = rotated[g * nocc : g * nocc + 8, lanes]
                    for r in range(1, nocc // 8):
                        at = g * nocc + r * 8
                        picked = jnp.where(bands[r], rotated[at : at + 8, lanes], picked)
                    row = jnp.sum(jnp.where(on_diag, picked, 0.0), axis=0, keepdims=True)
                    block = jnp.where(row8 == g, row, block)
                at = pl.multiple_of(shift + owner * chol_dev + c * STEP, 8)
                diag[pl.ds(at, STEP), (base + t) * 128 : (base + t) * 128 + 128] = block
            return tuple(out)

        sums = (zero,) * tiles
        for owner in owners:
            sums = lax.fori_loop(0, chol_dev // STEP, functools.partial(chunk, owner), sums, unroll=True)
        for t in range(tiles):
            diag[pl.ds(energy_row, 8), (base + t) * 128 : (base + t) * 128 + 128] = sums[t]
        return tiles

    def tabulate(chips, base):
        tiles = (len(chips) + 1) // 2
        lanes = diag[:, base * 128 : (base + tiles) * 128]
        table = jnp.sum(lanes.T.reshape(2 * tiles, nocc, 128), axis=1)
        for t, q in enumerate(chips):
            row = table[t : t + 1, :]
            if t == len(chips) - 1 and t % 2 == 0:
                row = row + jnp.where(is_energy, table[t + 1 : t + 2, :], 0.0)
            message[q + 1, :, :] = row

    @pl.when(side == 0)
    def _():
        pl.semaphore_wait(pair_ready, 1)
        to_partner.start()

    for j in range(depth):

        @pl.when(j > z)
        def _():
            pl.semaphore_wait(line_ready.at[j], 1)
            to_line[j].start()

    room = jnp.minimum(z, depth - 1 - z)
    onward = jnp.where(z > depth - 1 - z, -1, 1)
    others = []
    for t in range(1, depth):
        near_j = z - (t + 1) // 2 if t % 2 else z + t // 2
        others.append(jnp.where(t <= 2 * room, near_j, z + onward * (t - room)))
    for j in others[:1]:
        slot = slot_of(j, side)
        arrived(slot)
        walker_to(slot, pair_send.at[j], partner).start()
        sent.pop()

    owners = [core, 1 - core]
    load_chol.wait()
    await_copy(chol.at[1 - core], chol_recv.at[0])
    arrived(slot_of(z, 1 - side))
    base = compute([own, slot_of(z, 1 - side)], 0, owners)
    tabulate([chip, 2 * z + 1 - side], 0)

    for j in others[1:]:
        slot = slot_of(j, side)
        arrived(slot)
        walker_to(slot, pair_send.at[j], partner).start()
        sent.pop()

    for s in (side, 1 - side):
        whole = depth - 1 - LAST * (s is not side)
        cuts = [others[at : min(at + TILE, whole)] for at in range(0, whole, TILE)] + [others[whole:]]
        for js in filter(None, cuts):
            if s is not side:
                for j in js:
                    arrived(slot_of(j, s))
                if js[-1] is others[-1]:
                    beside = (chip + half + 1 - 2 * core) % half
                    remote(
                        walkers.at[slot_of(beside // 2, 1 - side)],
                        near_by.at[2 - 2 * core],
                        core_send.at[2],
                        near_recv.at[1],
                        sibling,
                    ).start()
            tiles = compute([slot_of(j, s) for j in js], base, owners)
            tabulate([2 * j + s for j in js], base)
            base += tiles
    message[0, :, :] = message[half, :, :]
    message[half + 1, :, :] = message[1, :, :]

    moved = len(sent)
    for k in range(1, n):
        target = (me + k) % n
        behind = (target + core) % 2
        row = target // 2 + 1 - behind * (1 - target % 2)
        remote(
            message.at[pl.ds(row, 2)], inbox.at[me], mail_send.at[k], mail_recv.at[me], target
        ).start()
    inbox[pl.ds(me, 1)] = message[pl.ds(chip + 1, 2)][None]

    near_by[1] = walkers[own]
    await_copy(near_by.at[0], near_recv.at[0])
    await_copy(near_by.at[0], near_recv.at[1])

    load_source.wait()
    load_counts.wait()
    my_count = counts[me]
    slots = reloc_ref.shape[0]
    chosen = []
    for s in range(slots):
        near = lax.rem(jnp.clip(source[s], 0, n - 1) - me + 1 + n, n)
        near = jnp.minimum(near, NEAR - 1)
        live = s < my_count
        value = near_by[near]
        reloc_ref[s] = jnp.where(live, value, jnp.zeros_like(value))
        chosen.append((near, live))

    def wait_sent(copies):
        for copy, when in copies:
            if when is None:
                copy.wait_send()
            else:
                pl.when(when)(copy.wait_send)

    wait_sent(sent[:moved])
    for k in range(1, n):
        origin = (me + k) % n
        await_copy(inbox.at[origin], mail_recv.at[origin])

    for s, (near, live) in enumerate(chosen):
        holder = jnp.where(near == 1, core, 1 - core)
        row_of = near // 2
        energy = jnp.zeros((1, 128), jnp.float32)
        for b in range(half // per):
            row = jnp.zeros((1, 128), jnp.float32)
            for q in range(per):
                got = inbox[(b * per + q) * 2 + holder, row_of]
                row = jnp.where(lane1 // (2 * chol_dev) == q, got, row)
                rest = (lane1 + (128 - (q + 1) * 2 * chol_dev)) % 128
                energy = energy + jnp.where(rest < 8, got, 0.0)
            bias_ref[s : s + 1, b * 128 : b * 128 + 128] = jnp.where(live, row, 0.0)
        energy_ref[s] = jnp.where(live, jnp.sum(energy) * (-0.5 / nchol), 0.0)

    wait_sent(sent[moved:])


def store(reloc_ref, energy_ref, bias_ref, reloc_out, energy_out, bias_out, sems):
    pairs = ((reloc_ref, reloc_out), (energy_ref, energy_out), (bias_ref, bias_out))
    copies = [pltpu.make_async_copy(src, dst, sems.at[i]) for i, (src, dst) in enumerate(pairs)]
    for copy in copies:
        copy.start()
    for copy in copies:
        copy.wait()


def body(greens, source, counts, cholesky):
    n = lax.axis_size("walk")
    chol_dev, nocc, orbitals = cholesky.shape
    slots = source.shape[0]
    nchol = chol_dev * n
    assert greens.shape[0] == 1 and nocc == 64 and chol_dev == 32
    depth = n // 4
    half = n // 2
    results = pl.pallas_call(
        functools.partial(kernel, n, nocc, chol_dev, nchol),
        out_shape=(
            pltpu.VMEM((slots, nocc, orbitals), jnp.bfloat16),
            pltpu.SMEM((slots,), jnp.float32),
            pltpu.VMEM((slots, nchol), jnp.float32),
        ),
        in_specs=[
            pl.BlockSpec(memory_space=pl.ANY),
            pl.BlockSpec(memory_space=pl.ANY),
            pl.BlockSpec(memory_space=pl.ANY),
            pl.BlockSpec(memory_space=pl.ANY),
        ],
        out_specs=(
            pl.BlockSpec(memory_space=pltpu.VMEM),
            pl.BlockSpec(memory_space=pltpu.SMEM),
            pl.BlockSpec(memory_space=pltpu.VMEM),
        ),
        scratch_shapes=[
            pltpu.SMEM((slots,), jnp.int32),
            pltpu.SMEM(counts.shape, jnp.int32),
            pltpu.VMEM((half, nocc, orbitals), jnp.bfloat16),
            pltpu.VMEM((2, chol_dev * nocc, orbitals), jnp.bfloat16),
            pltpu.VMEM((NEAR, nocc, orbitals), jnp.bfloat16),
            pltpu.VMEM((128, (2 + 2 * (depth // 2)) * 128), jnp.float32),
            pltpu.VMEM((half + 2, 1, 128), jnp.float32),
            pltpu.VMEM((n, 2, 1, 128), jnp.float32),
            pltpu.SemaphoreType.DMA((4,)),
            pltpu.SemaphoreType.REGULAR((depth,)),
            pltpu.SemaphoreType.REGULAR,
            pltpu.SemaphoreType.DMA((depth,)),
            pltpu.SemaphoreType.DMA((depth + 1,)),
            pltpu.SemaphoreType.DMA((3,)),
            pltpu.SemaphoreType.DMA((1,)),
            pltpu.SemaphoreType.DMA((half,)),
            pltpu.SemaphoreType.DMA((2,)),
            pltpu.SemaphoreType.DMA((n,)),
            pltpu.SemaphoreType.DMA((n,)),
        ],
        compiler_params=pltpu.CompilerParams(collective_id=0, has_side_effects=True),
    )(source, counts, greens.reshape(nocc, orbitals), cholesky.reshape(chol_dev * nocc, orbitals))
    places = (pltpu.VMEM, pltpu.SMEM, pltpu.VMEM)
    return pl.pallas_call(
        store,
        out_shape=tuple(jax.ShapeDtypeStruct(x.shape, x.dtype) for x in results),
        in_specs=[pl.BlockSpec(memory_space=m) for m in places],
        out_specs=(pl.BlockSpec(memory_space=pl.ANY),) * 3,
        scratch_shapes=[pltpu.SemaphoreType.DMA((3,))],
    )(*[pltpu.with_memory_space_constraint(x, m) for x, m in zip(results, places)])


def solution(mesh):
    return jax.shard_map(
        body,
        mesh=mesh,
        in_specs=(
            P(("rep", "walk"), None, None),
            P(("rep", "walk")),
            P("rep"),
            P("walk", None, None),
        ),
        out_specs=(P(("rep", "walk"), None, None), P(("rep", "walk")), P(("rep", "walk"), None)),
        check_vma=False,
    )
```
